32 devices in a mesh: section: 4 (over y, x), seq: 8 (over z, core).
Axes of the slice: x: 2, y: 2, z: 4, core: 2. Of those that a mesh axis runs over, the one named last changes fastest.
Arguments:
- teacher_query_array: bfloat16 [4, 2048, 4096], P('section', 'seq'), may hold values from -8 to 8
- teacher_keys: bfloat16 [4, 2048, 512], P('section', 'seq'), may hold values from -8 to 8
- teacher_value_array: bfloat16 [4, 2048, 512], P('section', 'seq'), may hold values from -6 to 6
- projection: bfloat16 [4, 8, 512, 128], P('section'), may hold values from -0.25 to 0.25
- student_query_array: bfloat16 [4, 1024, 2048], P('section', 'seq'), may hold values from -8 to 8
- student_keys: bfloat16 [4, 1024, 512], P('section', 'seq'), may hold values from -8 to 8
- student_value_array: bfloat16 [4, 1024, 512], P('section', 'seq'), may hold values from -6 to 6
Outputs:
- grad_student_q: float32 [4, 1024, 2048], P('section', 'seq')
- grad_student_keys: float32 [4, 1024, 512], P('section', 'seq')
- grad_student_values: float32 [4, 1024, 512], P('section', 'seq')
- per_token_loss: float32 [4, 1024], P('section', 'seq')
The draws below stay inside these ranges and needn't reach their ends.
All inputs are finite; a program needn't handle non-finite values.
Results may differ from the reference program's by a relative error of at most 0.03.
Values may be sent and summed in bfloat16 or wider, within the bound.
No kernel may reach another device: no remote copies, remote signals or barrier semaphores. Data moves between devices by JAX's collectives and lax.ppermute only.
A program may use at most 128 MiB of HBM per device.

```python
import math
import jax
import jax.numpy as jnp
from jax import lax

TOK_DEV = 256
HEAD_SIZE = 128
TEACHER_Q_HEADS = 64
TEACHER_KV_HEADS = 8
STUDENT_Q_HEADS = 16
STUDENT_KV_HEADS = 4
LAYER_PAIRS = 2
TOKEN_COUNT = 2048
N_SEQ = 8


def drawn_draw(key, salt_value, tensor_shape):
    drawn = jax.random.normal(jax.random.fold_in(key, salt_value), tensor_shape, dtype=jnp.float32)
    return jnp.clip(drawn, -4.0, 4.0)


def with_positions(key, salt_value, drawn):
    entries, rows, width = drawn.shape
    heads = width // HEAD_SIZE
    pairs = HEAD_SIZE // 8
    half_rows = TOK_DEV // 2
    row_ids = jnp.arange(rows, dtype=jnp.int32)
    entry_ids = jnp.arange(entries, dtype=jnp.int32)
    position = (TOK_DEV * (row_ids // half_rows))[None, :] + (half_rows * (entry_ids % 2))[:, None] + (row_ids % half_rows)[None, :]
    window = TOK_DEV / 8.0
    strength = math.log(4.0 * TOKEN_COUNT / TOK_DEV)
    amplitude = math.sqrt(strength * math.sqrt(HEAD_SIZE) / pairs)
    rates = jax.random.uniform(jax.random.fold_in(key, 9101), (entries // 2, pairs), dtype=jnp.float32, minval=0.05, maxval=1.0) * (math.pi / window)
    rates = jnp.repeat(rates, 2, axis=0)
    phases = position.astype(jnp.float32)[:, :, None] * rates[:, None, :]
    waves = jnp.concatenate([jnp.cos(phases), jnp.sin(phases)], -1)
    wobble = jax.random.uniform(jax.random.fold_in(key, salt_value), (entries, rows, heads, 2 * pairs), dtype=jnp.float32, minval=0.85, maxval=1.15)
    positional = waves[:, :, None, :] * amplitude * wobble
    grid = drawn.reshape(entries, rows, heads, HEAD_SIZE)
    grid = jnp.concatenate([grid[..., :HEAD_SIZE - 2 * pairs], positional], -1)
    return grid.reshape(entries, rows, width)


def draw_teacher_query_array(key, part):
    tensor_shape = (2 * LAYER_PAIRS, TOKEN_COUNT, TEACHER_Q_HEADS // 2 * HEAD_SIZE)
    drawn = drawn_draw(key, 101, tensor_shape)
    return drawn.astype(jnp.bfloat16)


def draw_teacher_keys(key, part):
    tensor_shape = (2 * LAYER_PAIRS, TOKEN_COUNT, TEACHER_KV_HEADS // 2 * HEAD_SIZE)
    drawn = drawn_draw(key, 102, tensor_shape)
    return drawn.astype(jnp.bfloat16)


def draw_student_query_array(key, part):
    tensor_shape = (2 * LAYER_PAIRS, TOKEN_COUNT // 2, STUDENT_Q_HEADS * HEAD_SIZE)
    drawn = with_positions(key, 9201, drawn_draw(key, 103, tensor_shape))
    return drawn.astype(jnp.bfloat16)


def draw_student_keys(key, part):
    tensor_shape = (2 * LAYER_PAIRS, TOKEN_COUNT // 2, STUDENT_KV_HEADS * HEAD_SIZE)
    drawn = with_positions(key, 9202, drawn_draw(key, 104, tensor_shape))
    return drawn.astype(jnp.bfloat16)


def steps_of(own_key, extent, shards, least, high):
    factor_of = 1.0
    for dim, blocks in shards:
        draws = jax.random.uniform(jax.random.fold_in(jax.random.fold_in(own_key, 6), dim), (blocks,), jnp.float32, least / len(shards), high / len(shards))
        factor_of = factor_of * jnp.repeat(jnp.exp(draws), extent[dim] // blocks).reshape((-1,) + (1,) * (len(extent) - 1 - dim))
    return factor_of


def noise(rng, shape, spread, most, split=(), kind=jnp.bfloat16):
    factor_of = steps_of(rng, shape, split, -0.22, 0.18) if split else 1.0
    result = jax.random.normal(rng, shape, jnp.float32) * spread * factor_of
    return jnp.minimum(jnp.maximum(result, -most), most).astype(kind)


def setup_inputs(seed: int = 0) -> dict:
    streams_of = jax.random.split(jax.random.key(seed), 8)
    return {
        "teacher_query_array": draw_teacher_query_array(jax.random.fold_in(streams_of[7], 71), 0),
        "teacher_keys": draw_teacher_keys(jax.random.fold_in(streams_of[7], 71), 0),
        "teacher_value_array": noise(streams_of[2], (2 * LAYER_PAIRS, TOKEN_COUNT, (TEACHER_KV_HEADS // 2) * HEAD_SIZE), 1.0, 6.0, ((0, 4), (1, 8))),
        "projection": noise(streams_of[3], (2 * LAYER_PAIRS, STUDENT_Q_HEADS // 2, (TEACHER_Q_HEADS // STUDENT_Q_HEADS) * HEAD_SIZE, HEAD_SIZE), ((TEACHER_Q_HEADS // STUDENT_Q_HEADS) * HEAD_SIZE) ** -0.5, 0.25, ((0, 4),)),
        "student_query_array": draw_student_query_array(jax.random.fold_in(streams_of[7], 71), 0),
        "student_keys": draw_student_keys(jax.random.fold_in(streams_of[7], 71), 0),
        "student_value_array": noise(streams_of[6], (2 * LAYER_PAIRS, TOKEN_COUNT // 2, STUDENT_KV_HEADS * HEAD_SIZE), 1.0, 6.0, ((0, 4), (1, 8))),
    }


floor_score = -1e+30

def reverted(operand):
    return lax.optimization_barrier(operand.astype(jnp.bfloat16)).astype(jnp.float32)

def causal_scores(queries, key_grid, query_pos, key_pos):
    scores = jnp.einsum('qgjd,kgd->gjqk', queries.astype(jnp.float32), key_grid.astype(jnp.float32)) * (1.0 / math.sqrt(HEAD_SIZE))
    allowed = key_pos[None, None, None, :] <= query_pos[None, None, :, None]
    return (jnp.where(allowed, scores, floor_score), allowed)

def softmax_parts(scores, allowed):
    row_peak = lax.optimization_barrier(jnp.max(scores, axis=-1))
    weights = jnp.where(allowed, jnp.exp(scores - row_peak[..., None]), 0.0)
    row_total = lax.optimization_barrier(jnp.sum(weights, axis=-1))
    return (row_peak, weights, row_total)

def attend(weights, row_total, value_grid):
    mixed = jnp.einsum('gjqk,kgd->qgjd', reverted(weights), value_grid.astype(jnp.float32))
    return mixed / jnp.transpose(row_total, (2, 0, 1))[..., None]

def teacher_context(queries, key_rows, value_rows):
    heads_of_keys = TEACHER_KV_HEADS
    heads_per_group = TEACHER_Q_HEADS // TEACHER_KV_HEADS
    rows_per_block = math.gcd(TOKEN_COUNT, 256)
    key_grid = key_rows.reshape(TOKEN_COUNT, heads_of_keys, HEAD_SIZE)
    value_grid = value_rows.reshape(TOKEN_COUNT, heads_of_keys, HEAD_SIZE)
    key_pos = jnp.arange(TOKEN_COUNT, dtype=jnp.int32)

    def query_block(block_index):
        offset = (block_index * rows_per_block).astype(jnp.int32)
        block_queries = lax.dynamic_slice_in_dim(queries, offset, rows_per_block, 0).reshape(rows_per_block, heads_of_keys, heads_per_group, HEAD_SIZE)
        query_pos = offset + jnp.arange(rows_per_block, dtype=jnp.int32)
        scores, allowed = causal_scores(block_queries, key_grid, query_pos, key_pos)
        row_peak, weights, row_total = softmax_parts(scores, allowed)
        return attend(weights, row_total, value_grid).astype(jnp.bfloat16).reshape(rows_per_block, TEACHER_Q_HEADS * HEAD_SIZE)
    blocks = lax.map(query_block, jnp.arange(TOKEN_COUNT // rows_per_block, dtype=jnp.int32))
    return blocks.reshape(TOKEN_COUNT, TEACHER_Q_HEADS * HEAD_SIZE)

def student_layer(queries, key_rows, value_rows, target):
    heads_of_keys = STUDENT_KV_HEADS
    heads_per_group = STUDENT_Q_HEADS // STUDENT_KV_HEADS
    rows_per_block = math.gcd(TOKEN_COUNT, 256)
    key_grid = key_rows.reshape(TOKEN_COUNT, heads_of_keys, HEAD_SIZE)
    value_grid = value_rows.reshape(TOKEN_COUNT, heads_of_keys, HEAD_SIZE)
    key_pos = jnp.arange(TOKEN_COUNT, dtype=jnp.int32)
    inverse_root = 1.0 / math.sqrt(HEAD_SIZE)

    def query_block(carried, block_index):
        key_gradient, value_gradient = carried
        offset = (block_index * rows_per_block).astype(jnp.int32)
        block_queries = lax.dynamic_slice_in_dim(queries, offset, rows_per_block, 0).reshape(rows_per_block, heads_of_keys, heads_per_group, HEAD_SIZE)
        query_pos = offset + jnp.arange(rows_per_block, dtype=jnp.int32)
        scores, allowed = causal_scores(block_queries, key_grid, query_pos, key_pos)
        row_peak, weights, row_total = softmax_parts(scores, allowed)
        context = attend(weights, row_total, value_grid)
        block_target = lax.dynamic_slice_in_dim(target, offset, rows_per_block, 0).reshape(rows_per_block, heads_of_keys, heads_per_group, HEAD_SIZE).astype(jnp.float32)
        mismatch = context - block_target
        per_token_loss = lax.optimization_barrier(jnp.mean(jnp.square(mismatch).reshape(rows_per_block, -1), axis=1))
        grad_context = reverted(mismatch)
        row_delta = jnp.transpose(lax.optimization_barrier(jnp.sum(mismatch * context, axis=-1)), (1, 2, 0))
        probability = jnp.where(allowed, jnp.exp(scores - row_peak[..., None]) / row_total[..., None], 0.0)
        grad_prob = jnp.einsum('qgjd,kgd->gjqk', grad_context, value_grid.astype(jnp.float32))
        grad_score = reverted(probability * (grad_prob - row_delta[..., None]))
        query_gradient = jnp.einsum('gjqk,kgd->qgjd', grad_score, key_grid.astype(jnp.float32)) * inverse_root
        key_gradient = key_gradient + jnp.einsum('gjqk,qgjd->kgd', grad_score, block_queries.astype(jnp.float32)) * inverse_root
        value_gradient = value_gradient + jnp.einsum('gjqk,qgjd->kgd', reverted(probability), grad_context)
        return ((key_gradient, value_gradient), (query_gradient.reshape(rows_per_block, STUDENT_Q_HEADS * HEAD_SIZE), per_token_loss))
    start_grads = (jnp.zeros((TOKEN_COUNT, heads_of_keys, HEAD_SIZE), jnp.float32), jnp.zeros((TOKEN_COUNT, heads_of_keys, HEAD_SIZE), jnp.float32))
    finals, outputs = lax.scan(query_block, start_grads, jnp.arange(TOKEN_COUNT // rows_per_block, dtype=jnp.int32))
    key_gradient, value_gradient = finals
    query_gradient, per_token_loss = outputs
    return (query_gradient.reshape(TOKEN_COUNT, STUDENT_Q_HEADS * HEAD_SIZE), key_gradient.reshape(TOKEN_COUNT, STUDENT_KV_HEADS * HEAD_SIZE), value_gradient.reshape(TOKEN_COUNT, STUDENT_KV_HEADS * HEAD_SIZE), per_token_loss.reshape(TOKEN_COUNT))

def reference(teacher_query_array, teacher_keys, teacher_value_array, projection, student_query_array, student_keys, student_value_array):
    rows_half = TOKEN_COUNT // 2 // N_SEQ

    def teacher_join(operand):
        return operand.reshape(LAYER_PAIRS, 2, TOKEN_COUNT, -1).transpose(0, 2, 1, 3).reshape(LAYER_PAIRS, TOKEN_COUNT, -1)

    def student_join(operand):
        return operand.reshape(LAYER_PAIRS, 2, N_SEQ, rows_half, -1).transpose(0, 2, 1, 3, 4).reshape(LAYER_PAIRS, TOKEN_COUNT, -1)

    def student_split(operand):
        return operand.reshape(LAYER_PAIRS, N_SEQ, 2, rows_half, -1).transpose(0, 2, 1, 3, 4).reshape(2 * LAYER_PAIRS, TOKEN_COUNT // 2, -1)
    queries_of_teacher = teacher_join(teacher_query_array)
    teacher_key_rows = teacher_join(teacher_keys)
    teacher_value_rows = teacher_join(teacher_value_array)
    queries_of_student = student_join(student_query_array)
    student_key_rows = student_join(student_keys)
    student_value_rows = student_join(student_value_array)
    maps = projection.reshape(LAYER_PAIRS, STUDENT_Q_HEADS, TEACHER_Q_HEADS // STUDENT_Q_HEADS * HEAD_SIZE, HEAD_SIZE)
    results = []
    for layer_index in range(LAYER_PAIRS):
        context = teacher_context(queries_of_teacher[layer_index], teacher_key_rows[layer_index], teacher_value_rows[layer_index])
        target = jnp.einsum('thf,hfe->the', context.reshape(TOKEN_COUNT, STUDENT_Q_HEADS, -1).astype(jnp.float32), maps[layer_index].astype(jnp.float32))
        target = target.astype(jnp.bfloat16).reshape(TOKEN_COUNT, STUDENT_Q_HEADS * HEAD_SIZE)
        results.append(student_layer(queries_of_student[layer_index], student_key_rows[layer_index], student_value_rows[layer_index], target))
    query_gradient = student_split(jnp.stack([entry[0] for entry in results]))
    key_gradient = student_split(jnp.stack([entry[1] for entry in results]))
    value_gradient = student_split(jnp.stack([entry[2] for entry in results]))
    per_token_loss = student_split(jnp.stack([entry[3] for entry in results])[..., None])[..., 0]
    return (query_gradient, key_gradient, value_gradient, per_token_loss)
```

```python
import functools
import math

import jax
import jax.numpy as jnp
from jax import lax
from jax.experimental import pallas as pl
from jax.experimental.pallas import tpu as pltpu
from jax.sharding import PartitionSpec as P

HEAD = 128
TEACHER_Q_HEADS = 64
TEACHER_KV_HEADS = 8
STUDENT_Q_HEADS = 16
STUDENT_KV_HEADS = 4
GROUP_T = TEACHER_Q_HEADS // TEACHER_KV_HEADS
GROUP_S = STUDENT_Q_HEADS // STUDENT_KV_HEADS
PER_TARGET = TEACHER_Q_HEADS // STUDENT_Q_HEADS

floor_score = -1e30
inverse_root = 1.0 / math.sqrt(HEAD)
exp2_scale = inverse_root * math.log2(math.e)
vmem_limit = 60 * 1024 * 1024


def dot(left, right):
    return lax.dot_general(
        left, right, (((1,), (0,)), ((), ())), preferred_element_type=jnp.float32
    )


def shift(value, chips, least=0):
    size = lax.axis_size("seq")
    pairs = [(i, i + 2 * chips) for i in range(2 * least, size - 2 * chips)]
    return lax.ppermute(value, "seq", pairs)


def back(value, chips):
    size = lax.axis_size("seq")
    pairs = [(i, i - 2 * chips) for i in range(2 * chips, size)]
    return lax.ppermute(value, "seq", pairs)


def swap(value, axis):
    pairs = [(i, i ^ 1) for i in range(lax.axis_size(axis))]
    return lax.ppermute(value, axis, pairs)


def spread(own):
    chips = lax.axis_size("seq") // 2
    mine = [own]
    for step in range(1, chips):
        if step <= 2:
            mine.append(shift(own, step))
        else:
            mine.append(shift(mine[-1], 1, step - 1))
    return [(block, swap(block, "seq")) for block in mine]


def fold_max(tile):
    return jnp.max(tile.reshape(-1, 8, tile.shape[1]), axis=0)


def fold_sum(tile):
    return jnp.sum(tile.reshape(-1, 8, tile.shape[1]), axis=0)


def teacher_kernel(chips, rows, info, q_ref, *refs):
    key_refs = refs[: 2 * chips]
    value_refs = refs[2 * chips : 4 * chips]
    proj_ref, out_ref = refs[4 * chips : 4 * chips + 2]
    keys, values_t, query_t, scores, total, context = refs[4 * chips + 2 :]
    chip, core = info[0], info[1]
    wide = 2 * rows
    for b in range(chips):
        for half in range(2):
            part = pl.ds(half * rows, rows)
            keys[b, part, :] = key_refs[2 * b + half][...]
            values_t[b, :, part] = value_refs[2 * b + half][...].T
    for h in range(GROUP_T):
        query_t[h] = q_ref[:, h * HEAD : (h + 1) * HEAD].T

    key_id = lax.broadcasted_iota(jnp.int32, (wide, rows), 0)
    row_id = lax.broadcasted_iota(jnp.int32, (wide, rows), 1)
    ahead = jnp.where(key_id < rows, key_id, key_id + (1 - 2 * core) * rows - rows)
    allowed = ahead <= row_id

    def score(h, slot, b, peak, diagonal):
        tile = dot(keys[b], query_t[h])
        if diagonal:
            tile = jnp.where(allowed, tile, floor_score)
        scores[slot, b] = tile
        return jnp.maximum(peak, fold_max(tile))

    def absorb(slot, b, shifted, row_sum, first):
        weights = jnp.exp2(scores[slot, b] * exp2_scale - shifted)
        added = dot(values_t[b], weights.astype(jnp.bfloat16))
        total[...] = added if first else total[...] + added
        return row_sum + fold_sum(weights)

    def reduced(peak):
        return jnp.max(peak, axis=0, keepdims=True) * exp2_scale

    def finish(h, row_sum):
        denominator = jnp.sum(row_sum, axis=0, keepdims=True)
        start = pl.multiple_of(h * HEAD, HEAD)
        context[pl.ds(start, HEAD), :] = (total[...] / denominator).astype(jnp.bfloat16)

    low = jnp.full((8, rows), floor_score, jnp.float32)
    none = jnp.zeros((8, rows), jnp.float32)

    peak = score(0, 0, 0, low, True)
    peak = lax.fori_loop(1, chip + 1, lambda b, p: score(0, 0, b, p, False), peak)

    def head(h, peak):
        slot = lax.rem(h, 2)
        shifted = reduced(peak)
        new_peak = score(h, slot, 0, low, True)
        row_sum = absorb(1 - slot, 0, shifted, none, True)

        def block(b, carried):
            new_peak, row_sum = carried
            new_peak = score(h, slot, b, new_peak, False)
            row_sum = absorb(1 - slot, b, shifted, row_sum, False)
            return new_peak, row_sum

        new_peak, row_sum = lax.fori_loop(1, chip + 1, block, (new_peak, row_sum))
        finish(h - 1, row_sum)
        return new_peak

    peak = lax.fori_loop(1, GROUP_T, head, peak)
    shifted = reduced(peak)
    slot = (GROUP_T - 1) % 2
    row_sum = absorb(slot, 0, shifted, none, True)
    row_sum = lax.fori_loop(
        1, chip + 1, lambda b, r: absorb(slot, b, shifted, r, False), row_sum
    )
    finish(GROUP_T - 1, row_sum)
    deep = PER_TARGET * HEAD
    for t in range(GROUP_T // PER_TARGET):
        made = dot(proj_ref[t].T, context[t * deep : (t + 1) * deep, :])
        out_ref[t * HEAD : (t + 1) * HEAD, :] = made.astype(jnp.bfloat16)


def teacher(info, queries, blocks, projection, first_head, heads):
    chips = len(blocks)
    rows = queries.shape[0]
    flat = [part for pair in blocks for part in pair]
    targets = GROUP_T // PER_TARGET
    in_specs = [pl.BlockSpec((rows, GROUP_T * HEAD), lambda g, i: (0, first_head + g))]
    in_specs += [pl.BlockSpec((rows, HEAD), lambda g, i: (0, g))] * len(flat)
    in_specs += [pl.BlockSpec((rows, HEAD), lambda g, i: (0, heads + g))] * len(flat)
    in_specs += [
        pl.BlockSpec(
            (targets, PER_TARGET * HEAD, HEAD), lambda g, i: (first_head + g, 0, 0)
        )
    ]
    wide = 2 * rows
    work = heads * GROUP_T * rows * chips * wide
    return pl.pallas_call(
        functools.partial(teacher_kernel, chips, rows),
        out_shape=jax.ShapeDtypeStruct((heads * targets * HEAD, rows), jnp.bfloat16),
        grid_spec=pltpu.PrefetchScalarGridSpec(
            num_scalar_prefetch=1,
            grid=(heads,),
            in_specs=in_specs,
            out_specs=pl.BlockSpec((targets * HEAD, rows), lambda g, i: (g, 0)),
            scratch_shapes=[
                pltpu.VMEM((chips, wide, HEAD), jnp.bfloat16),
                pltpu.VMEM((chips, HEAD, wide), jnp.bfloat16),
                pltpu.VMEM((GROUP_T, HEAD, rows), jnp.bfloat16),
                pltpu.VMEM((2, chips, wide, rows), jnp.float32),
                pltpu.VMEM((HEAD, rows), jnp.float32),
                pltpu.VMEM((GROUP_T * HEAD, rows), jnp.bfloat16),
            ],
        ),
        compiler_params=pltpu.CompilerParams(
            dimension_semantics=("arbitrary",), vmem_limit_bytes=vmem_limit
        ),
        cost_estimate=pl.CostEstimate(
            flops=4 * HEAD * work, bytes_accessed=4 * wide * HEAD * chips, transcendentals=work
        ),
        name="teacher",
    )(info, queries, *flat, *flat, projection)


def student_kernel(chips, rows, info, own_q_ref, far_q_ref, target_ref, *refs):
    key_refs = refs[: 2 * chips]
    value_refs = refs[2 * chips : 4 * chips]
    near_ref, away_ref, loss_ref, kept_ref, sent_ref = refs[4 * chips : 4 * chips + 5]
    (
        keys,
        keys_t,
        values,
        values_t,
        query,
        query_t,
        scores,
        total,
        key_sum,
        value_sum,
        query_sum,
        loss_sum,
    ) = refs[4 * chips + 5 :]
    chip, core, bit = info[0], info[1], info[2]
    wide = 2 * rows
    half_rows = rows // 2
    for b in range(chips):
        for half in range(2):
            part = pl.ds(half * rows, rows)
            key_block = key_refs[2 * b + half][...]
            value_block = value_refs[2 * b + half][...]
            keys[b, part, :] = key_block
            keys_t[b, :, part] = key_block.T
            values[b, part, :] = value_block
            values_t[b, :, part] = value_block.T
    mine = pl.ds(pl.multiple_of(bit * half_rows, half_rows), half_rows)
    other = pl.ds(pl.multiple_of((1 - bit) * half_rows, half_rows), half_rows)
    for h in range(GROUP_S):
        query[h, mine, :] = own_q_ref[:, h * HEAD : (h + 1) * HEAD]
        query[h, other, :] = far_q_ref[:, h * HEAD : (h + 1) * HEAD]
    for h in range(GROUP_S):
        query_t[h] = query[h].T

    key_id = lax.broadcasted_iota(jnp.int32, (wide, rows), 0)
    row_id = lax.broadcasted_iota(jnp.int32, (wide, rows), 1)
    within = lax.rem(key_id, rows)
    place = jnp.where(within < half_rows, within + bit * half_rows, within - bit * half_rows)
    ahead = jnp.where(key_id < rows, place, place + (1 - 2 * core) * rows)
    allowed = ahead <= row_id

    low = jnp.full((8, rows), floor_score, jnp.float32)
    none = jnp.zeros((8, rows), jnp.float32)
    loss_sum[...] = jnp.zeros_like(loss_sum)

    def head(h, first):
        def score(b, peak, diagonal):
            tile = dot(keys[b], query_t[h])
            if diagonal:
                tile = jnp.where(allowed, tile, floor_score)
            scores[b] = tile
            return jnp.maximum(peak, fold_max(tile))

        peak = score(0, low, True)
        peak = lax.fori_loop(1, chip + 1, lambda b, p: score(b, p, False), peak)
        shifted = jnp.max(peak, axis=0, keepdims=True) * exp2_scale

        def absorb(b, row_sum, first):
            weights = jnp.exp2(scores[b] * exp2_scale - shifted)
            scores[b] = weights
            added = dot(values_t[b], weights.astype(jnp.bfloat16))
            total[...] = added if first else total[...] + added
            return row_sum + fold_sum(weights)

        row_sum = absorb(0, none, True)
        row_sum = lax.fori_loop(1, chip + 1, lambda b, r: absorb(b, r, False), row_sum)
        inverse = 1.0 / jnp.sum(row_sum, axis=0, keepdims=True)
        made = total[...] * inverse
        start = pl.multiple_of(h * HEAD, HEAD)
        mismatch = made - target_ref[pl.ds(start, HEAD), :].astype(jnp.float32)
        loss_sum[...] += fold_sum(jnp.square(mismatch))
        delta = jnp.sum(mismatch * made, axis=0, keepdims=True)
        grad_t = mismatch.astype(jnp.bfloat16)
        grad = mismatch.T.astype(jnp.bfloat16)

        def gradient(b, start):
            prob = scores[b] * inverse
            grad_prob = dot(values[b], grad_t)
            grad_score = (prob * (grad_prob - delta)).astype(jnp.bfloat16)
            added = dot(keys_t[b], grad_score)
            total[...] = added if start else total[...] + added
            key_added = dot(grad_score, query[h])
            value_added = dot(prob.astype(jnp.bfloat16), grad)
            if first:
                key_sum[b] = key_added
                value_sum[b] = value_added
            else:
                key_sum[b] += key_added
                value_sum[b] += value_added

        gradient(0, True)
        lax.fori_loop(1, chip + 1, lambda b, c: (gradient(b, False), c)[1], 0)
        query_sum[h] = (total[...] * inverse_root).T

    head(0, True)
    lax.fori_loop(1, GROUP_S, lambda h, c: (head(h, False), c)[1], 0)
    for h in range(GROUP_S):
        near_ref[:, h * HEAD : (h + 1) * HEAD] = query_sum[h, mine, :]
        away_ref[:, h * HEAD : (h + 1) * HEAD] = query_sum[h, other, :].astype(jnp.bfloat16)
    loss_ref[...] = loss_sum[...]
    for b in range(chips):

        @pl.when(b <= chip)
        def _():
            kept_ref[b, :, :HEAD] = key_sum[b, :rows, :] * inverse_root
            kept_ref[b, :, HEAD:] = value_sum[b, :rows, :]
            sent_ref[b, :, :HEAD] = (key_sum[b, rows:, :] * inverse_root).astype(jnp.bfloat16)
            sent_ref[b, :, HEAD:] = value_sum[b, rows:, :].astype(jnp.bfloat16)


def student(info, own_queries, far_queries, target, blocks, pair, heads):
    chips = len(blocks)
    rows = blocks[0][0].shape[0]
    half_rows = rows // 2
    wide = 2 * rows
    flat = [part for both in blocks for part in both]
    width = GROUP_S * HEAD
    full = lambda i, info: (0, 0)
    in_specs = [
        pl.BlockSpec((half_rows, width), lambda i, info: (0, info[2] * heads + pair)),
        pl.BlockSpec((half_rows, width), lambda i, info: (0, pair)),
        pl.BlockSpec((width, rows), full),
    ]
    in_specs += [pl.BlockSpec((rows, HEAD), lambda i, info: (0, pair))] * len(flat)
    in_specs += [pl.BlockSpec((rows, HEAD), lambda i, info: (0, heads + pair))] * len(flat)
    work = GROUP_S * rows * chips * wide
    return pl.pallas_call(
        functools.partial(student_kernel, chips, rows),
        out_shape=(
            jax.ShapeDtypeStruct((half_rows, width), jnp.float32),
            jax.ShapeDtypeStruct((half_rows, width), jnp.bfloat16),
            jax.ShapeDtypeStruct((8, rows), jnp.float32),
            jax.ShapeDtypeStruct((chips, rows, 2 * HEAD), jnp.float32),
            jax.ShapeDtypeStruct((chips, rows, 2 * HEAD), jnp.bfloat16),
        ),
        grid_spec=pltpu.PrefetchScalarGridSpec(
            num_scalar_prefetch=1,
            grid=(1,),
            in_specs=in_specs,
            out_specs=(
                pl.BlockSpec((half_rows, width), full),
                pl.BlockSpec((half_rows, width), full),
                pl.BlockSpec((8, rows), full),
                pl.BlockSpec((chips, rows, 2 * HEAD), lambda i, info: (0, 0, 0)),
                pl.BlockSpec((chips, rows, 2 * HEAD), lambda i, info: (0, 0, 0)),
            ),
            scratch_shapes=[
                pltpu.VMEM((chips, wide, HEAD), jnp.bfloat16),
                pltpu.VMEM((chips, HEAD, wide), jnp.bfloat16),
                pltpu.VMEM((chips, wide, HEAD), jnp.bfloat16),
                pltpu.VMEM((chips, HEAD, wide), jnp.bfloat16),
                pltpu.VMEM((GROUP_S, rows, HEAD), jnp.bfloat16),
                pltpu.VMEM((GROUP_S, HEAD, rows), jnp.bfloat16),
                pltpu.VMEM((chips, wide, rows), jnp.float32),
                pltpu.VMEM((HEAD, rows), jnp.float32),
                pltpu.VMEM((chips, wide, HEAD), jnp.float32),
                pltpu.VMEM((chips, wide, HEAD), jnp.float32),
                pltpu.VMEM((GROUP_S, rows, HEAD), jnp.float32),
                pltpu.VMEM((8, rows), jnp.float32),
            ],
        ),
        compiler_params=pltpu.CompilerParams(
            dimension_semantics=("arbitrary",), vmem_limit_bytes=vmem_limit
        ),
        cost_estimate=pl.CostEstimate(
            flops=12 * HEAD * work, bytes_accessed=8 * wide * HEAD * chips, transcendentals=work
        ),
        name="student",
    )(info, own_queries, far_queries, target, *flat, *flat)


def body(
    teacher_query_array,
    teacher_keys,
    teacher_value_array,
    projection,
    student_query_array,
    student_keys,
    student_value_array,
):
    bit = lax.axis_index("section") % 2
    seq = lax.axis_index("seq")
    chips = lax.axis_size("seq") // 2
    info = jnp.stack([seq // 2, seq % 2, bit]).astype(jnp.int32)
    teacher_heads = TEACHER_KV_HEADS // 2
    student_heads = STUDENT_KV_HEADS // 2
    per_pair = teacher_heads // student_heads
    rows = teacher_keys.shape[1]
    half_rows = rows // 2

    def columns(array, which, width):
        return lax.dynamic_slice_in_dim(array, which * width, width, 1)

    kv_width = student_heads * HEAD
    q_width = STUDENT_Q_HEADS // 2 * HEAD
    own_q = student_query_array[0]

    def pair_rows(which):
        return jnp.concatenate(
            [
                columns(student_keys[0], which, kv_width),
                columns(student_value_array[0], which, kv_width),
            ],
            1,
        )

    student_rows = jnp.concatenate([pair_rows(bit), swap(pair_rows(1 - bit), "section")], 0)
    far_q = swap(columns(own_q, 1 - bit, q_width), "section")

    def teacher_rows(pair):
        part = slice(pair * per_pair * HEAD, (pair + 1) * per_pair * HEAD)
        return jnp.concatenate([teacher_keys[0][:, part], teacher_value_array[0][:, part]], 1)

    teacher_blocks = [spread(teacher_rows(0))]
    student_blocks = spread(student_rows)
    for pair in range(1, student_heads):
        teacher_blocks.append(spread(teacher_rows(pair)))

    query_own, query_far, key_own, key_far, loss = [], [], [], [], 0.0
    for pair in range(student_heads):
        target = teacher(
            info,
            teacher_query_array[0],
            teacher_blocks[pair],
            projection[0],
            pair * per_pair,
            per_pair,
        )
        near, away, squares, kept, sent = student(
            info, own_q, far_q, target, student_blocks, pair, student_heads
        )
        query_own.append(near)
        query_far.append(swap(away, "section").astype(jnp.float32))
        loss = loss + jnp.sum(squares, axis=0)
        terms = kept + swap(sent, "seq").astype(jnp.float32)
        summed = terms[0]
        for step in range(1, chips):
            summed = summed + back(terms[step].astype(jnp.bfloat16), step).astype(jnp.float32)
        far = swap(summed[half_rows:].astype(jnp.bfloat16), "section").astype(jnp.float32)
        key_own.append(summed[:half_rows])
        key_far.append(far)

    def arrange(own, far):
        return jnp.where(
            bit == 0,
            jnp.concatenate(own + far, 1),
            jnp.concatenate(far + own, 1),
        )

    grad_q = arrange(query_own, query_far)
    grad_k = arrange([x[:, :HEAD] for x in key_own], [x[:, :HEAD] for x in key_far])
    grad_v = arrange([x[:, HEAD:] for x in key_own], [x[:, HEAD:] for x in key_far])
    halves = loss.reshape(2, half_rows)
    mine = jnp.where(bit == 0, halves[0], halves[1])
    theirs = jnp.where(bit == 0, halves[1], halves[0])
    token_loss = (mine + swap(theirs, "section")) / (STUDENT_Q_HEADS * HEAD)
    return grad_q[None], grad_k[None], grad_v[None], token_loss[None]


def solution(mesh):
    in_specs = (
        P("section", "seq", None),
        P("section", "seq", None),
        P("section", "seq", None),
        P("section", None, None, None),
        P("section", "seq", None),
        P("section", "seq", None),
        P("section", "seq", None),
    )
    out_specs = (
        P("section", "seq", None),
        P("section", "seq", None),
        P("section", "seq", None),
        P("section", "seq"),
    )
    return jax.shard_map(body, mesh=mesh, in_specs=in_specs, out_specs=out_specs, check_vma=False)
```

```python
import functools
import math

import jax
import jax.numpy as jnp
from jax import lax
from jax.experimental import pallas as pl
from jax.experimental.pallas import tpu as pltpu
from jax.sharding import PartitionSpec as P


HEAD = 128
TEACHER_Q_HEADS = 64
TEACHER_KV_HEADS = 8
STUDENT_Q_HEADS = 16
STUDENT_KV_HEADS = 4
GROUP_T = TEACHER_Q_HEADS // TEACHER_KV_HEADS
GROUP_S = STUDENT_Q_HEADS // STUDENT_KV_HEADS
PER_TARGET = TEACHER_Q_HEADS // STUDENT_Q_HEADS

floor_score = -1e30
inverse_root = 1.0 / math.sqrt(HEAD)
exp2_scale = inverse_root * math.log2(math.e)
vmem_limit = 60 * 1024 * 1024
chunk = 64
pace = 10000
piece = 512


def dot(left, right):
    return lax.dot_general(
        left, right, (((1,), (0,)), ((), ())), preferred_element_type=jnp.float32
    )


def shift(value, chips, least=0):
    size = lax.axis_size("seq")
    pairs = [(i, i + 2 * chips) for i in range(2 * least, size - 2 * chips)]
    return lax.ppermute(value, "seq", pairs)


def back(value, chips):
    size = lax.axis_size("seq")
    pairs = [(i, i - 2 * chips) for i in range(2 * chips, size)]
    return lax.ppermute(value, "seq", pairs)


def swap(value, axis):
    pairs = [(i, i ^ 1) for i in range(lax.axis_size(axis))]
    return lax.ppermute(value, axis, pairs)


def spread(own, relay):
    chips = lax.axis_size("seq") // 2
    mine = [own]
    for step in range(1, chips):
        if step <= 2 or not relay:
            mine.append(shift(own, step))
        else:
            mine.append(shift(mine[-1], 1, step - 1))
    return mine


def both_cores(mine):
    blocks = []
    for block in mine:
        blocks.append((block, swap(block, "seq")))
    return blocks


def variants(chips):
    return [*range(2, chips, 2), chips]


def fold_max(tile):
    return jnp.max(tile.reshape(-1, 8, tile.shape[1]), axis=0)


def fold_sum(tile):
    return jnp.sum(tile.reshape(-1, 8, tile.shape[1]), axis=0)


def paced(history, bound):
    if len(history) <= pace:
        return bound
    return jnp.maximum(bound, floor_score - history[-pace])


def weigh(scores, weights, start, size, peak, history, keep):
    row_sum = history[-1]
    for u in range(start, start + size, chunk):
        part = pl.ds(u, chunk)
        gap = scores[part, :].reshape(-1, 8, peak.shape[1]) - paced(history, peak)
        weight = jnp.exp2(gap * exp2_scale).reshape(chunk, peak.shape[1])
        if keep:
            scores[part, :] = weight
        weights[part, :] = weight.astype(jnp.bfloat16)
        row_sum = row_sum + fold_sum(weight)
        history.append(row_sum)


def spread_max(peak):
    return jnp.broadcast_to(jnp.max(peak, axis=0, keepdims=True), peak.shape)


def teacher_kernel(chips, rows, heads, info, q_ref, *refs):
    key_refs = refs[: 2 * chips]
    value_refs = refs[2 * chips : 4 * chips]
    proj_ref, out_ref, keys, values_t, query_t, *refs = refs[4 * chips :]
    scores, weights, (peaks, context) = refs[:2], refs[2:4], refs[4:]
    chip, core = info[0], info[1]
    wide = 2 * rows
    pairs = GROUP_T // 2
    for b in range(2 * chips):
        part = pl.ds(b * rows, rows)

        @pl.when(b < 2 * (chip + 2))
        def _():
            for g in range(heads):
                columns = slice(g * HEAD, (g + 1) * HEAD)
                keys[g, part, :] = key_refs[b][:, columns]
                values_t[g, :, part] = value_refs[b][:, columns].T

    for h in range(heads * GROUP_T):
        half = pl.ds(h % 2 * rows, rows)
        query_t[h // 2, :, half] = q_ref[:, h * HEAD : (h + 1) * HEAD].T

    key_id = lax.broadcasted_iota(jnp.int32, (wide, wide), 0)
    row_id = lax.broadcasted_iota(jnp.int32, (wide, wide), 1)
    row_id = jnp.where(row_id < rows, row_id, row_id - rows)
    ahead = jnp.where(key_id < rows, key_id, key_id + (1 - 2 * core) * rows - rows)
    allowed = ahead <= row_id

    def score(b, pair, slot, peak):
        part = pl.ds(b * wide, wide)
        tile = dot(keys[pair // pairs, part, :], query_t[pair])
        if b == 0:
            tile = jnp.where(allowed, tile, floor_score)
        scores[slot][part, :] = tile
        return jnp.maximum(peak, held(b, fold_max(tile), floor_score))

    def held(b, value, otherwise):
        return value if b == 0 else jnp.where(b <= chip, value, otherwise)

    low = jnp.full((8, wide), floor_score, jnp.float32)

    for least, count in zip([0, *variants(chips)], variants(chips)):

        @pl.when(jnp.logical_and(chip >= least, chip < count))
        def _():
            peak = low
            for b in range(count):
                peak = score(b, 0, 0, peak)
            peaks[...] = peak

            def step(pair, slot):
                later = jnp.minimum(pair + 1, heads * pairs - 1)
                top = spread_max(peaks[...])
                history = [jnp.zeros((8, wide), jnp.float32)]
                peak = low
                for b in range(count):
                    bound = held(b, top, -floor_score)
                    weigh(scores[slot], weights[slot], b * wide, wide, bound, history, False)
                    peak = score(b, later, 1 - slot, peak)
                end = count * wide
                mixed = dot(values_t[pair // pairs, :, :end], weights[slot][:end, :])
                mixed = mixed / jnp.sum(history[-1], axis=0, keepdims=True)
                for half in range(2):
                    start = pl.multiple_of((2 * pair + half) * HEAD, HEAD)
                    made = mixed[:, half * rows : (half + 1) * rows]
                    context[pl.ds(start, HEAD), :] = made.astype(jnp.bfloat16)
                peaks[...] = peak

            def two(i, carried):
                step(2 * i, 0)
                step(2 * i + 1, 1)
                return carried

            lax.fori_loop(0, heads * pairs // 2, two, 0)

    deep = PER_TARGET * HEAD
    for t in range(heads * GROUP_T // PER_TARGET):
        made = dot(proj_ref[t].T, context[t * deep : (t + 1) * deep, :])
        out_ref[t * HEAD : (t + 1) * HEAD, :] = made.astype(jnp.bfloat16)


def teacher(info, queries, blocks, projection, first_head, heads):
    chips = len(blocks)
    rows = queries.shape[0]
    flat = [part for pair in blocks for part in pair]
    targets = heads * GROUP_T // PER_TARGET
    turn = first_head // heads
    in_specs = [pl.BlockSpec((rows, heads * GROUP_T * HEAD), lambda i, info: (0, turn))]
    in_specs += [pl.BlockSpec((rows, heads * HEAD), lambda i, info: (0, 0))] * len(flat)
    in_specs += [pl.BlockSpec((rows, heads * HEAD), lambda i, info: (0, 1))] * len(flat)
    in_specs += [
        pl.BlockSpec((targets, PER_TARGET * HEAD, HEAD), lambda i, info: (turn, 0, 0))
    ]
    wide = 2 * rows
    work = heads * GROUP_T * rows * chips * wide
    return pl.pallas_call(
        functools.partial(teacher_kernel, chips, rows, heads),
        out_shape=jax.ShapeDtypeStruct((targets * HEAD, rows), jnp.bfloat16),
        grid_spec=pltpu.PrefetchScalarGridSpec(
            num_scalar_prefetch=1,
            grid=(1,),
            in_specs=in_specs,
            out_specs=pl.BlockSpec((targets * HEAD, rows), lambda i, info: (0, 0)),
            scratch_shapes=[
                pltpu.VMEM((heads, chips * wide, HEAD), jnp.bfloat16),
                pltpu.VMEM((heads, HEAD, chips * wide), jnp.bfloat16),
                pltpu.VMEM((heads * GROUP_T // 2, HEAD, wide), jnp.bfloat16),
                *[pltpu.VMEM((chips * wide, wide), jnp.float32)] * 2,
                *[pltpu.VMEM((chips * wide, wide), jnp.bfloat16)] * 2,
                pltpu.VMEM((8, wide), jnp.float32),
                pltpu.VMEM((heads * GROUP_T * HEAD, rows), jnp.bfloat16),
            ],
        ),
        compiler_params=pltpu.CompilerParams(
            dimension_semantics=("arbitrary",), vmem_limit_bytes=vmem_limit
        ),
        cost_estimate=pl.CostEstimate(
            flops=4 * HEAD * work, bytes_accessed=4 * wide * HEAD * chips, transcendentals=work
        ),
        name="teacher",
    )(info, queries, *flat, *flat, projection)


def student_kernel(chips, rows, info, own_q_ref, far_q_ref, target_ref, *refs):
    key_refs = refs[: 2 * chips]
    value_refs = refs[2 * chips : 4 * chips]
    near_ref, away_ref, loss_ref, kept_ref, sent_ref = refs[4 * chips : 4 * chips + 5]
    keys, keys_t, values, values_t, query, query_t, scores, weights = refs[
        4 * chips + 5 : 4 * chips + 13
    ]
    grad_scores, key_sum, value_sum, query_sum, loss_sum = refs[4 * chips + 13 :]
    chip, core, bit = info[0], info[1], info[2]
    wide = 2 * rows
    half_rows = rows // 2
    for b in range(2 * chips):
        part = pl.ds(b * rows, rows)

        @pl.when(b < 2 * (chip + 2))
        def _():
            key_block = key_refs[b][...]
            value_block = value_refs[b][...]
            keys[part, :] = key_block
            keys_t[:, part] = key_block.T
            values[part, :] = value_block
            values_t[:, part] = value_block.T
            key_sum[part, :] = jnp.zeros((rows, HEAD), jnp.float32)
            value_sum[part, :] = jnp.zeros((rows, HEAD), jnp.float32)

    mine = pl.multiple_of(bit * half_rows, half_rows)
    other = pl.multiple_of((1 - bit) * half_rows, half_rows)
    for h in range(GROUP_S):
        columns = slice(h * HEAD, (h + 1) * HEAD)
        base = h % 2 * rows
        query[h // 2, pl.ds(base + mine, half_rows), :] = own_q_ref[:, columns]
        query[h // 2, pl.ds(base + other, half_rows), :] = far_q_ref[:, columns]
    for p in range(GROUP_S // 2):
        query_t[p] = query[p].T

    key_id = lax.broadcasted_iota(jnp.int32, (wide, wide), 0)
    row_id = lax.broadcasted_iota(jnp.int32, (wide, wide), 1)
    row_id = jnp.where(row_id < rows, row_id, row_id - rows)
    within = jnp.where(key_id < rows, key_id, key_id - rows)
    place = jnp.where(within < half_rows, within + bit * half_rows, within - bit * half_rows)
    ahead = jnp.where(key_id < rows, place, place + (1 - 2 * core) * rows)
    allowed = ahead <= row_id
    loss_sum[...] = jnp.zeros_like(loss_sum)

    def held(b, value, otherwise):
        return value if b == 0 else jnp.where(b <= chip, value, otherwise)

    for least, count in zip([0, *variants(chips)], variants(chips)):

        @pl.when(jnp.logical_and(chip >= least, chip < count))
        def _():
            def step(pair, carried):
                end = count * wide
                peak = jnp.full((8, wide), floor_score, jnp.float32)
                for b in range(count):
                    part = pl.ds(b * wide, wide)
                    tile = dot(keys[part, :], query_t[pair])
                    if b == 0:
                        tile = jnp.where(allowed, tile, floor_score)
                    scores[part, :] = tile
                    peak = jnp.maximum(peak, held(b, fold_max(tile), floor_score))
                history = [jnp.zeros((8, wide), jnp.float32)]
                top = spread_max(peak)
                for b in range(count):
                    bound = held(b, top, -floor_score)
                    weigh(scores, weights, b * wide, wide, bound, history, True)
                inverse = 1.0 / jnp.sum(history[-1], axis=0, keepdims=True)
                made = dot(values_t[:, :end], weights[:end, :]) * inverse
                start = pl.multiple_of(pair * 2 * HEAD, 2 * HEAD)
                target = target_ref[pl.ds(start, 2 * HEAD), :].astype(jnp.float32)
                mismatch = made - jnp.concatenate([target[:HEAD], target[HEAD:]], 1)
                squares = fold_sum(jnp.square(mismatch))
                loss_sum[...] += squares[:, :rows] + squares[:, rows:]
                delta = jnp.sum(mismatch * made, axis=0, keepdims=True)
                grad_t = mismatch.astype(jnp.bfloat16)
                grad = mismatch.T.astype(jnp.bfloat16)
                for u in range(0, end, piece):
                    part = pl.ds(u, piece)
                    prob = scores[part, :] * inverse
                    grad_prob = dot(values[part, :], grad_t)
                    grad_score = (prob * (grad_prob - delta)).astype(jnp.bfloat16)
                    grad_scores[part, :] = grad_score
                    key_sum[part, :] += dot(grad_score, query[pair])
                    value_sum[part, :] += dot(prob.astype(jnp.bfloat16), grad)
                summed = dot(keys_t[:, :end], grad_scores[:end, :]) * inverse_root
                query_sum[2 * pair] = summed[:, :rows].T
                query_sum[2 * pair + 1] = summed[:, rows:].T
                return carried

            lax.fori_loop(0, GROUP_S // 2, step, 0)

    for h in range(GROUP_S):
        near_ref[:, h * HEAD : (h + 1) * HEAD] = query_sum[h, pl.ds(mine, half_rows), :]
        away_ref[:, h * HEAD : (h + 1) * HEAD] = query_sum[h, pl.ds(other, half_rows), :].astype(
            jnp.bfloat16
        )
    loss_ref[...] = jnp.sum(loss_sum[...], axis=0, keepdims=True)
    for b in range(chips):

        @pl.when(b <= chip)
        def _():
            own = pl.ds(b * wide, rows)
            far = pl.ds(b * wide + rows, rows)
            kept_ref[b, :, :HEAD] = key_sum[own, :] * inverse_root
            kept_ref[b, :, HEAD:] = value_sum[own, :]
            sent_ref[b, :, :HEAD] = (key_sum[far, :] * inverse_root).astype(jnp.bfloat16)
            sent_ref[b, :, HEAD:] = value_sum[far, :].astype(jnp.bfloat16)


def student(info, own_queries, far_queries, target, blocks, pair, heads):
    chips = len(blocks)
    rows = blocks[0][0].shape[0]
    half_rows = rows // 2
    wide = 2 * rows
    flat = [part for both in blocks for part in both]
    width = GROUP_S * HEAD
    full = lambda i, info: (0, 0)
    in_specs = [
        pl.BlockSpec((half_rows, width), lambda i, info: (0, info[2] * heads + pair)),
        pl.BlockSpec((half_rows, width), lambda i, info: (0, pair)),
        pl.BlockSpec((width, rows), full),
    ]
    in_specs += [pl.BlockSpec((rows, HEAD), lambda i, info: (0, 0))] * len(flat)
    in_specs += [pl.BlockSpec((rows, HEAD), lambda i, info: (0, 1))] * len(flat)
    work = GROUP_S * rows * chips * wide
    return pl.pallas_call(
        functools.partial(student_kernel, chips, rows),
        out_shape=(
            jax.ShapeDtypeStruct((half_rows, width), jnp.float32),
            jax.ShapeDtypeStruct((half_rows, width), jnp.bfloat16),
            jax.ShapeDtypeStruct((1, rows), jnp.float32),
            jax.ShapeDtypeStruct((chips, rows, 2 * HEAD), jnp.float32),
            jax.ShapeDtypeStruct((chips, rows, 2 * HEAD), jnp.bfloat16),
        ),
        grid_spec=pltpu.PrefetchScalarGridSpec(
            num_scalar_prefetch=1,
            grid=(1,),
            in_specs=in_specs,
            out_specs=(
                pl.BlockSpec((half_rows, width), full),
                pl.BlockSpec((half_rows, width), full),
                pl.BlockSpec((1, rows), full),
                pl.BlockSpec((chips, rows, 2 * HEAD), lambda i, info: (0, 0, 0)),
                pl.BlockSpec((chips, rows, 2 * HEAD), lambda i, info: (0, 0, 0)),
            ),
            scratch_shapes=[
                pltpu.VMEM((chips * wide, HEAD), jnp.bfloat16),
                pltpu.VMEM((HEAD, chips * wide), jnp.bfloat16),
                pltpu.VMEM((chips * wide, HEAD), jnp.bfloat16),
                pltpu.VMEM((HEAD, chips * wide), jnp.bfloat16),
                pltpu.VMEM((GROUP_S // 2, wide, HEAD), jnp.bfloat16),
                pltpu.VMEM((GROUP_S // 2, HEAD, wide), jnp.bfloat16),
                pltpu.VMEM((chips * wide, wide), jnp.float32),
                *[pltpu.VMEM((chips * wide, wide), jnp.bfloat16)] * 2,
                *[pltpu.VMEM((chips * wide, HEAD), jnp.float32)] * 2,
                pltpu.VMEM((GROUP_S, rows, HEAD), jnp.float32),
                pltpu.VMEM((8, rows), jnp.float32),
            ],
        ),
        compiler_params=pltpu.CompilerParams(
            dimension_semantics=("arbitrary",), vmem_limit_bytes=vmem_limit
        ),
        cost_estimate=pl.CostEstimate(
            flops=12 * HEAD * work, bytes_accessed=8 * wide * HEAD * chips, transcendentals=work
        ),
        name="student",
    )(info, own_queries, far_queries, target, *flat, *flat)


def program(
    teacher_query_array,
    teacher_keys,
    teacher_value_array,
    projection,
    student_query_array,
    student_keys,
    student_value_array,
):
    bit = lax.axis_index("section") % 2
    seq = lax.axis_index("seq")
    chips = lax.axis_size("seq") // 2
    info = jnp.stack([seq // 2, seq % 2, bit]).astype(jnp.int32)
    teacher_heads = TEACHER_KV_HEADS // 2
    student_heads = STUDENT_KV_HEADS // 2
    per_pair = teacher_heads // student_heads
    rows = teacher_keys.shape[1]
    half_rows = rows // 2

    def columns(array, which, width):
        return lax.dynamic_slice_in_dim(array, which * width, width, 1)

    kv_width = student_heads * HEAD
    q_width = STUDENT_Q_HEADS // 2 * HEAD
    own_q = student_query_array[0]

    def teacher_rows(pair):
        part = slice(pair * per_pair * HEAD, (pair + 1) * per_pair * HEAD)
        return jnp.concatenate([teacher_keys[0][:, part], teacher_value_array[0][:, part]], 1)

    def pair_rows(which):
        return jnp.concatenate(
            [
                columns(student_keys[0], which, kv_width),
                columns(student_value_array[0], which, kv_width),
            ],
            1,
        )

    teacher_mine = [spread(teacher_rows(0), False)]
    far_rows = swap(pair_rows(1 - bit), "section")
    student_rows = jnp.concatenate([pair_rows(bit), far_rows], 0)
    student_mine = []
    for pair in range(student_heads):
        if pair:
            teacher_mine.append(spread(teacher_rows(pair), False))
        key_part = student_rows[:, pair * HEAD : (pair + 1) * HEAD]
        value_part = student_rows[:, kv_width + pair * HEAD : kv_width + (pair + 1) * HEAD]
        student_mine.append(spread(jnp.concatenate([key_part, value_part], 1), False))
    far_q = swap(columns(own_q, 1 - bit, q_width), "section")

    query_own, query_far, key_own, key_far, loss = [], [], [], [], 0.0
    for pair in range(student_heads):
        blocks = both_cores(teacher_mine[pair])
        target = teacher(
            info, teacher_query_array[0], blocks, projection[0], pair * per_pair, per_pair
        )
        blocks = both_cores(student_mine[pair])
        near, away, squares, kept, sent = student(
            info, own_q, far_q, target, blocks, pair, student_heads
        )
        query_own.append(near)
        query_far.append(swap(away, "section"))
        loss = loss + squares[0]
        terms = kept + swap(sent, "seq").astype(jnp.float32)
        summed = terms[0]
        for step in range(1, chips):
            got = back(terms[step].astype(jnp.bfloat16), step)
            summed = summed + got.astype(jnp.float32)
        far = swap(summed[half_rows:].astype(jnp.bfloat16), "section")
        key_own.append(summed[:half_rows])
        key_far.append(far.astype(jnp.float32))
    query_far = [part.astype(jnp.float32) for part in query_far]

    def arrange(own, far):
        return jnp.where(
            bit == 0,
            jnp.concatenate(own + far, 1),
            jnp.concatenate(far + own, 1),
        )

    grad_q = arrange(query_own, query_far)
    grad_k = arrange([x[:, :HEAD] for x in key_own], [x[:, :HEAD] for x in key_far])
    grad_v = arrange([x[:, HEAD:] for x in key_own], [x[:, HEAD:] for x in key_far])
    halves = loss.reshape(2, half_rows)
    mine = jnp.where(bit == 0, halves[0], halves[1])
    theirs = jnp.where(bit == 0, halves[1], halves[0])
    got = swap(theirs, "section")
    token_loss = (mine + got) / (STUDENT_Q_HEADS * HEAD)
    return grad_q[None], grad_k[None], grad_v[None], token_loss[None]


def solution(mesh):
    in_specs = (
        P("section", "seq", None),
        P("section", "seq", None),
        P("section", "seq", None),
        P("section", None, None, None),
        P("section", "seq", None),
        P("section", "seq", None),
        P("section", "seq", None),
    )
    out_specs = (
        P("section", "seq", None),
        P("section", "seq", None),
        P("section", "seq", None),
        P("section", "seq"),
    )
    return jax.shard_map(
        program, mesh=mesh, in_specs=in_specs, out_specs=out_specs, check_vma=False
    )
```

```python
import functools
import math

import jax
import jax.numpy as jnp
from jax import lax
from jax.experimental import pallas as pl
from jax.experimental.pallas import tpu as pltpu
from jax.sharding import PartitionSpec as P


HEAD = 128
TEACHER_Q_HEADS = 64
TEACHER_KV_HEADS = 8
STUDENT_Q_HEADS = 16
STUDENT_KV_HEADS = 4
GROUP_T = TEACHER_Q_HEADS // TEACHER_KV_HEADS
GROUP_S = STUDENT_Q_HEADS // STUDENT_KV_HEADS
PER_TARGET = TEACHER_Q_HEADS // STUDENT_Q_HEADS

floor_score = -1e30
inverse_root = 1.0 / math.sqrt(HEAD)
exp2_scale = inverse_root * math.log2(math.e)
vmem_limit = 60 * 1024 * 1024
chunk = 64
pace = 10000
piece = 512


def dot(left, right):
    return lax.dot_general(
        left, right, (((1,), (0,)), ((), ())), preferred_element_type=jnp.float32
    )


def shift(value, chips, least=0):
    pairs = [(i, i + 2 * chips) for i in range(2 * least, lax.axis_size("seq") - 2 * chips)]
    return lax.ppermute(value, "seq", pairs)


def back(value, chips):
    size = lax.axis_size("seq")
    pairs = [(i, i - 2 * chips) for i in range(2 * chips, size)]
    return lax.ppermute(value, "seq", pairs)


def swap(value, axis):
    pairs = [(i, i ^ 1) for i in range(lax.axis_size(axis))]
    return lax.ppermute(value, axis, pairs)


def spread(own, relay=False):
    mine = [own]
    for step in range(1, lax.axis_size("seq") // 2):
        mine.append(shift(mine[-1], 1, step - 1) if relay else shift(own, step))
    return mine


def both_cores(mine):
    blocks = []
    for block in mine:
        blocks.append((block, swap(block, "seq")))
    return blocks


def variants(chips):
    return sorted({max(chips - 1, 1), chips})


def fold_max(tile):
    return jnp.max(tile.reshape(-1, 8, tile.shape[1]), axis=0)


def fold_sum(tile):
    return jnp.sum(tile.reshape(-1, 8, tile.shape[1]), axis=0)


def paced(history, bound):
    if len(history) <= pace:
        return bound
    return jnp.maximum(bound, floor_score - history[-pace])


def weigh(scores, weights, start, size, peak, history, keep):
    row_sum = history[-1]
    for u in range(start, start + size, chunk):
        part = pl.ds(u, chunk)
        gap = scores[part, :].reshape(-1, 8, peak.shape[1]) - paced(history, peak)
        weight = jnp.exp2(gap * exp2_scale).reshape(chunk, peak.shape[1])
        if keep:
            scores[part, :] = weight
        weights[part, :] = weight.astype(jnp.bfloat16)
        row_sum = row_sum + fold_sum(weight)
        history.append(row_sum)


def spread_max(peak):
    return jnp.broadcast_to(jnp.max(peak, axis=0, keepdims=True), peak.shape)


def teacher_kernel(chips, rows, heads, info, q_ref, *refs):
    key_refs = refs[: 2 * chips]
    value_refs = refs[2 * chips : 4 * chips]
    proj_ref, out_ref, keys, values_t, query_t, *refs = refs[4 * chips :]
    scores, weights, (peaks, context) = refs[:2], refs[2:4], refs[4:]
    chip, core = info[0], info[1]
    wide = 2 * rows
    pairs = GROUP_T // 2
    for b in range(2 * chips):
        part = pl.ds(b * rows, rows)

        @pl.when(b < 2 * jnp.maximum(chip + 1, chips - 1))
        def _():
            for g in range(heads):
                columns = slice(g * HEAD, (g + 1) * HEAD)
                keys[g, part, :] = key_refs[b][:, columns]
                values_t[g, :, part] = value_refs[b][:, columns].T

    for h in range(heads * GROUP_T):
        half = pl.ds(h % 2 * rows, rows)
        query_t[h // 2, :, half] = q_ref[:, h * HEAD : (h + 1) * HEAD].T

    key_id = lax.broadcasted_iota(jnp.int32, (wide, wide), 0)
    row_id = lax.broadcasted_iota(jnp.int32, (wide, wide), 1)
    row_id = jnp.where(row_id < rows, row_id, row_id - rows)
    ahead = jnp.where(key_id < rows, key_id, key_id + (1 - 2 * core) * rows - rows)
    allowed = ahead <= row_id

    def score(b, pair, slot, peak):
        part = pl.ds(b * wide, wide)
        tile = dot(keys[pair // pairs, part, :], query_t[pair])
        if b == 0:
            tile = jnp.where(allowed, tile, floor_score)
        scores[slot][part, :] = tile
        return jnp.maximum(peak, held(b, fold_max(tile), floor_score))

    def held(b, value, otherwise):
        return value if b == 0 else jnp.where(b <= chip, value, otherwise)

    low = jnp.full((8, wide), floor_score, jnp.float32)

    for least, count in zip([0, *variants(chips)], variants(chips)):

        @pl.when(jnp.logical_and(chip >= least, chip < count))
        def _():
            peak = low
            for b in range(count):
                peak = score(b, 0, 0, peak)
            peaks[...] = peak

            def step(pair, slot):
                later = jnp.minimum(pair + 1, heads * pairs - 1)
                top = spread_max(peaks[...])
                history = [jnp.zeros((8, wide), jnp.float32)]
                peak = low
                for b in range(count):
                    bound = held(b, top, -floor_score)
                    weigh(scores[slot], weights[slot], b * wide, wide, bound, history, False)
                    peak = score(b, later, 1 - slot, peak)
                end = count * wide
                mixed = dot(values_t[pair // pairs, :, :end], weights[slot][:end, :])
                mixed = mixed / jnp.sum(history[-1], axis=0, keepdims=True)
                for half in range(2):
                    start = pl.multiple_of((2 * pair + half) * HEAD, HEAD)
                    made = mixed[:, half * rows : (half + 1) * rows]
                    context[pl.ds(start, HEAD), :] = made.astype(jnp.bfloat16)
                peaks[...] = peak

            def two(i, carried):
                step(2 * i, 0)
                step(2 * i + 1, 1)
                return carried

            lax.fori_loop(0, heads * pairs // 2, two, 0)

    deep = PER_TARGET * HEAD
    for t in range(heads * GROUP_T // PER_TARGET):
        made = dot(proj_ref[t].T, context[t * deep : (t + 1) * deep, :])
        out_ref[t * HEAD : (t + 1) * HEAD, :] = made.astype(jnp.bfloat16)


def teacher(info, queries, blocks, projection, first_head, heads):
    chips = len(blocks)
    rows = queries.shape[0]
    flat = [part for pair in blocks for part in pair]
    targets = heads * GROUP_T // PER_TARGET
    turn = first_head // heads
    in_specs = [pl.BlockSpec((rows, heads * GROUP_T * HEAD), lambda i, info: (0, turn))]
    in_specs += [pl.BlockSpec((rows, heads * HEAD), lambda i, info: (0, 0))] * len(flat)
    in_specs += [pl.BlockSpec((rows, heads * HEAD), lambda i, info: (0, 1))] * len(flat)
    in_specs += [
        pl.BlockSpec((targets, PER_TARGET * HEAD, HEAD), lambda i, info: (turn, 0, 0))
    ]
    wide = 2 * rows
    work = heads * GROUP_T * rows * chips * wide
    return pl.pallas_call(
        functools.partial(teacher_kernel, chips, rows, heads),
        out_shape=jax.ShapeDtypeStruct((targets * HEAD, rows), jnp.bfloat16),
        grid_spec=pltpu.PrefetchScalarGridSpec(
            num_scalar_prefetch=1,
            grid=(1,),
            in_specs=in_specs,
            out_specs=pl.BlockSpec((targets * HEAD, rows), lambda i, info: (0, 0)),
            scratch_shapes=[
                pltpu.VMEM((heads, chips * wide, HEAD), jnp.bfloat16),
                pltpu.VMEM((heads, HEAD, chips * wide), jnp.bfloat16),
                pltpu.VMEM((heads * GROUP_T // 2, HEAD, wide), jnp.bfloat16),
                *[pltpu.VMEM((chips * wide, wide), jnp.float32)] * 2,
                *[pltpu.VMEM((chips * wide, wide), jnp.bfloat16)] * 2,
                pltpu.VMEM((8, wide), jnp.float32),
                pltpu.VMEM((heads * GROUP_T * HEAD, rows), jnp.bfloat16),
            ],
        ),
        compiler_params=pltpu.CompilerParams(
            dimension_semantics=("arbitrary",), vmem_limit_bytes=vmem_limit
        ),
        cost_estimate=pl.CostEstimate(
            flops=4 * HEAD * work, bytes_accessed=4 * wide * HEAD * chips, transcendentals=work
        ),
        name="teacher",
    )(info, queries, *flat, *flat, projection)


def student_kernel(chips, rows, info, own_q_ref, far_q_ref, target_ref, *refs):
    key_refs = refs[: 2 * chips]
    value_refs = refs[2 * chips : 4 * chips]
    near_ref, away_ref, loss_ref, kept_ref, sent_ref = refs[4 * chips : 4 * chips + 5]
    keys, keys_t, values, values_t, query, query_t, scores, weights = refs[
        4 * chips + 5 : 4 * chips + 13
    ]
    grad_scores, key_sum, value_sum, query_sum, loss_sum = refs[4 * chips + 13 :]
    chip, core, bit = info[0], info[1], info[2]
    wide = 2 * rows
    half_rows = rows // 2
    for b in range(2 * chips):
        part = pl.ds(b * rows, rows)

        @pl.when(b < 2 * jnp.maximum(chip + 1, chips - 1))
        def _():
            key_block = key_refs[b][...]
            value_block = value_refs[b][...]
            keys[part, :] = key_block
            keys_t[:, part] = key_block.T
            values[part, :] = value_block
            values_t[:, part] = value_block.T
            key_sum[part, :] = jnp.zeros((rows, HEAD), jnp.float32)
            value_sum[part, :] = jnp.zeros((rows, HEAD), jnp.float32)

    mine = pl.multiple_of(bit * half_rows, half_rows)
    other = pl.multiple_of((1 - bit) * half_rows, half_rows)
    for h in range(GROUP_S):
        columns = slice(h * HEAD, (h + 1) * HEAD)
        base = h % 2 * rows
        query[h // 2, pl.ds(base + mine, half_rows), :] = own_q_ref[:, columns]
        query[h // 2, pl.ds(base + other, half_rows), :] = far_q_ref[:, columns]
    for p in range(GROUP_S // 2):
        query_t[p] = query[p].T

    key_id = lax.broadcasted_iota(jnp.int32, (wide, wide), 0)
    row_id = lax.broadcasted_iota(jnp.int32, (wide, wide), 1)
    row_id = jnp.where(row_id < rows, row_id, row_id - rows)
    within = jnp.where(key_id < rows, key_id, key_id - rows)
    place = jnp.where(within < half_rows, within + bit * half_rows, within - bit * half_rows)
    ahead = jnp.where(key_id < rows, place, place + (1 - 2 * core) * rows)
    allowed = ahead <= row_id
    loss_sum[...] = jnp.zeros_like(loss_sum)

    def held(b, value, otherwise):
        return value if b == 0 else jnp.where(b <= chip, value, otherwise)

    for least, count in zip([0, *variants(chips)], variants(chips)):

        @pl.when(jnp.logical_and(chip >= least, chip < count))
        def _():
            def step(pair, carried):
                end = count * wide
                peak = jnp.full((8, wide), floor_score, jnp.float32)
                for b in range(count):
                    part = pl.ds(b * wide, wide)
                    tile = dot(keys[part, :], query_t[pair])
                    if b == 0:
                        tile = jnp.where(allowed, tile, floor_score)
                    scores[part, :] = tile
                    peak = jnp.maximum(peak, held(b, fold_max(tile), floor_score))
                history = [jnp.zeros((8, wide), jnp.float32)]
                top = spread_max(peak)
                for b in range(count):
                    bound = held(b, top, -floor_score)
                    weigh(scores, weights, b * wide, wide, bound, history, True)
                inverse = 1.0 / jnp.sum(history[-1], axis=0, keepdims=True)
                made = dot(values_t[:, :end], weights[:end, :]) * inverse
                start = pl.multiple_of(pair * 2 * HEAD, 2 * HEAD)
                target = target_ref[pl.ds(start, 2 * HEAD), :].astype(jnp.float32)
                mismatch = made - jnp.concatenate([target[:HEAD], target[HEAD:]], 1)
                squares = fold_sum(jnp.square(mismatch))
                loss_sum[...] += squares[:, :rows] + squares[:, rows:]
                delta = jnp.sum(mismatch * made, axis=0, keepdims=True)
                grad_t = mismatch.astype(jnp.bfloat16)
                grad = mismatch.T.astype(jnp.bfloat16)
                for u in range(0, end, piece):
                    part = pl.ds(u, piece)
                    prob = scores[part, :] * inverse
                    grad_prob = dot(values[part, :], grad_t)
                    grad_score = (prob * (grad_prob - delta)).astype(jnp.bfloat16)
                    grad_scores[part, :] = grad_score
                    key_sum[part, :] += dot(grad_score, query[pair])
                    value_sum[part, :] += dot(prob.astype(jnp.bfloat16), grad)
                summed = dot(keys_t[:, :end], grad_scores[:end, :]) * inverse_root
                query_sum[2 * pair] = summed[:, :rows].T
                query_sum[2 * pair + 1] = summed[:, rows:].T
                return carried

            lax.fori_loop(0, GROUP_S // 2, step, 0)

    for h in range(GROUP_S):
        near_ref[:, h * HEAD : (h + 1) * HEAD] = query_sum[h, pl.ds(mine, half_rows), :]
        away_ref[:, h * HEAD : (h + 1) * HEAD] = query_sum[h, pl.ds(other, half_rows), :].astype(
            jnp.bfloat16
        )
    loss_ref[...] = jnp.sum(loss_sum[...], axis=0, keepdims=True)
    for b in range(chips):

        @pl.when(b <= chip)
        def _():
            own = pl.ds(b * wide, rows)
            far = pl.ds(b * wide + rows, rows)
            kept_ref[b, :, :HEAD] = key_sum[own, :] * inverse_root
            kept_ref[b, :, HEAD:] = value_sum[own, :]
            sent_ref[b, :, :HEAD] = (key_sum[far, :] * inverse_root).astype(jnp.bfloat16)
            sent_ref[b, :, HEAD:] = value_sum[far, :].astype(jnp.bfloat16)


def student(info, own_queries, far_queries, target, blocks, pair, heads):
    chips = len(blocks)
    rows = blocks[0][0].shape[0]
    half_rows = rows // 2
    wide = 2 * rows
    flat = [part for both in blocks for part in both]
    width = GROUP_S * HEAD
    full = lambda i, info: (0, 0)
    in_specs = [
        pl.BlockSpec((half_rows, width), lambda i, info: (0, info[2] * heads + pair)),
        pl.BlockSpec((half_rows, width), lambda i, info: (0, pair)),
        pl.BlockSpec((width, rows), full),
    ]
    in_specs += [pl.BlockSpec((rows, HEAD), lambda i, info: (0, pair))] * len(flat)
    in_specs += [pl.BlockSpec((rows, HEAD), lambda i, info: (0, heads + pair))] * len(flat)
    work = GROUP_S * rows * chips * wide
    return pl.pallas_call(
        functools.partial(student_kernel, chips, rows),
        out_shape=(
            jax.ShapeDtypeStruct((half_rows, width), jnp.float32),
            jax.ShapeDtypeStruct((half_rows, width), jnp.bfloat16),
            jax.ShapeDtypeStruct((1, rows), jnp.float32),
            jax.ShapeDtypeStruct((chips, rows, 2 * HEAD), jnp.float32),
            jax.ShapeDtypeStruct((chips, rows, 2 * HEAD), jnp.bfloat16),
        ),
        grid_spec=pltpu.PrefetchScalarGridSpec(
            num_scalar_prefetch=1,
            grid=(1,),
            in_specs=in_specs,
            out_specs=(
                pl.BlockSpec((half_rows, width), full),
                pl.BlockSpec((half_rows, width), full),
                pl.BlockSpec((1, rows), full),
                pl.BlockSpec((chips, rows, 2 * HEAD), lambda i, info: (0, 0, 0)),
                pl.BlockSpec((chips, rows, 2 * HEAD), lambda i, info: (0, 0, 0)),
            ),
            scratch_shapes=[
                pltpu.VMEM((chips * wide, HEAD), jnp.bfloat16),
                pltpu.VMEM((HEAD, chips * wide), jnp.bfloat16),
                pltpu.VMEM((chips * wide, HEAD), jnp.bfloat16),
                pltpu.VMEM((HEAD, chips * wide), jnp.bfloat16),
                pltpu.VMEM((GROUP_S // 2, wide, HEAD), jnp.bfloat16),
                pltpu.VMEM((GROUP_S // 2, HEAD, wide), jnp.bfloat16),
                pltpu.VMEM((chips * wide, wide), jnp.float32),
                *[pltpu.VMEM((chips * wide, wide), jnp.bfloat16)] * 2,
                *[pltpu.VMEM((chips * wide, HEAD), jnp.float32)] * 2,
                pltpu.VMEM((GROUP_S, rows, HEAD), jnp.float32),
                pltpu.VMEM((8, rows), jnp.float32),
            ],
        ),
        compiler_params=pltpu.CompilerParams(
            dimension_semantics=("arbitrary",), vmem_limit_bytes=vmem_limit
        ),
        cost_estimate=pl.CostEstimate(
            flops=12 * HEAD * work, bytes_accessed=8 * wide * HEAD * chips, transcendentals=work
        ),
        name="student",
    )(info, own_queries, far_queries, target, *flat, *flat)


def program(
    teacher_query_array,
    teacher_keys,
    teacher_value_array,
    projection,
    student_query_array,
    student_keys,
    student_value_array,
):
    bit = lax.axis_index("section") % 2
    seq = lax.axis_index("seq")
    chips = lax.axis_size("seq") // 2
    info = jnp.stack([seq // 2, seq % 2, bit]).astype(jnp.int32)
    teacher_heads = TEACHER_KV_HEADS // 2
    student_heads = STUDENT_KV_HEADS // 2
    per_pair = teacher_heads // student_heads
    rows = teacher_keys.shape[1]
    half_rows = rows // 2

    def columns(array, which, width):
        return lax.dynamic_slice_in_dim(array, which * width, width, 1)

    kv_width = student_heads * HEAD
    q_width = STUDENT_Q_HEADS // 2 * HEAD
    own_q = student_query_array[0]

    def teacher_rows(pair):
        part = slice(pair * per_pair * HEAD, (pair + 1) * per_pair * HEAD)
        return jnp.concatenate([teacher_keys[0][:, part], teacher_value_array[0][:, part]], 1)

    def pair_rows(which):
        return jnp.concatenate(
            [
                columns(student_keys[0], which, kv_width),
                columns(student_value_array[0], which, kv_width),
            ],
            1,
        )

    far_rows = swap(pair_rows(1 - bit), "section")
    student_all = jnp.concatenate([pair_rows(bit), far_rows], 0)

    chunks = [spread(teacher_rows(pair), pair == 0) for pair in range(student_heads)]
    student_mine = spread(student_all)
    far_q = swap(columns(own_q, 1 - bit, q_width), "section")

    targets = []
    for pair in range(student_heads):
        blocks = both_cores(chunks[pair])
        made = teacher(
            info, teacher_query_array[0], blocks, projection[0], pair * per_pair, per_pair
        )
        targets.append(made)
    student_blocks = both_cores(student_mine)

    query_own, query_far, key_own, key_far, loss = [], [], [], [], 0.0
    for pair in range(student_heads):
        near, away, squares, kept, sent = student(
            info, own_q, far_q, targets[pair], student_blocks, pair, student_heads
        )
        query_own.append(near)
        query_far.append(swap(away, "section"))
        loss = loss + squares[0]
        terms = kept + swap(sent, "seq").astype(jnp.float32)
        summed = terms[0]
        for step in range(1, chips):
            got = back(terms[step].astype(jnp.bfloat16), step)
            summed = summed + got.astype(jnp.float32)
        far = swap(summed[half_rows:].astype(jnp.bfloat16), "section")
        key_own.append(summed[:half_rows])
        key_far.append(far.astype(jnp.float32))
    query_far = [part.astype(jnp.float32) for part in query_far]

    def arrange(own, far):
        return jnp.where(
            bit == 0,
            jnp.concatenate(own + far, 1),
            jnp.concatenate(far + own, 1),
        )

    grad_q = arrange(query_own, query_far)
    grad_k = arrange([x[:, :HEAD] for x in key_own], [x[:, :HEAD] for x in key_far])
    grad_v = arrange([x[:, HEAD:] for x in key_own], [x[:, HEAD:] for x in key_far])
    halves = loss.reshape(2, half_rows)
    mine = jnp.where(bit == 0, halves[0], halves[1])
    theirs = jnp.where(bit == 0, halves[1], halves[0])
    got = swap(theirs, "section")
    token_loss = (mine + got) / (STUDENT_Q_HEADS * HEAD)
    return grad_q[None], grad_k[None], grad_v[None], token_loss[None]


def solution(mesh):
    in_specs = (
        P("section", "seq", None),
        P("section", "seq", None),
        P("section", "seq", None),
        P("section", None, None, None),
        P("section", "seq", None),
        P("section", "seq", None),
        P("section", "seq", None),
    )
    out_specs = (
        P("section", "seq", None),
        P("section", "seq", None),
        P("section", "seq", None),
        P("section", "seq"),
    )
    return jax.shard_map(
        program, mesh=mesh, in_specs=in_specs, out_specs=out_specs, check_vma=False
    )
```

```python
import functools
import math

import jax
import jax.numpy as jnp
from jax import lax
from jax.experimental import pallas as pl
from jax.experimental.pallas import tpu as pltpu
from jax.sharding import PartitionSpec as P


HEAD = 128
TEACHER_Q_HEADS = 64
TEACHER_KV_HEADS = 8
STUDENT_Q_HEADS = 16
STUDENT_KV_HEADS = 4
GROUP_T = TEACHER_Q_HEADS // TEACHER_KV_HEADS
GROUP_S = STUDENT_Q_HEADS // STUDENT_KV_HEADS
PER_TARGET = TEACHER_Q_HEADS // STUDENT_Q_HEADS

floor_score = -1e30
inverse_root = 1.0 / math.sqrt(HEAD)
exp2_scale = inverse_root * math.log2(math.e)
vmem_limit = 60 * 1024 * 1024
chunk = 64
piece = 512


def dot(left, right):
    return lax.dot_general(
        left, right, (((1,), (0,)), ((), ())), preferred_element_type=jnp.float32
    )


def shift(value, chips, least=0):
    pairs = [(i, i + 2 * chips) for i in range(2 * least, lax.axis_size("seq") - 2 * chips)]
    return lax.ppermute(value, "seq", pairs)


def back(value, chips):
    size = lax.axis_size("seq")
    pairs = [(i, i - 2 * chips) for i in range(2 * chips, size)]
    return lax.ppermute(value, "seq", pairs)


def swap(value, axis):
    pairs = [(i, i ^ 1) for i in range(lax.axis_size(axis))]
    return lax.ppermute(value, axis, pairs)


def spread(own, relay=False):
    mine = [own]
    for step in range(1, lax.axis_size("seq") // 2):
        mine.append(shift(mine[-1], 1, step - 1) if relay else shift(own, step))
    return mine


def both_cores(mine):
    blocks = []
    for block in mine:
        blocks.append((block, swap(block, "seq")))
    return blocks


def variants(chips):
    return sorted({max(chips - 1, 1), chips})


def fold_max(tile):
    return jnp.max(tile.reshape(-1, 8, tile.shape[1]), axis=0)


def fold_sum(tile):
    return jnp.sum(tile.reshape(-1, 8, tile.shape[1]), axis=0)


def paced(history, bound, pace):
    if pace is None or len(history) <= pace:
        return bound
    return jnp.maximum(bound, floor_score - history[-pace])


def weigh(scores, weights, start, size, peak, history, keep, pace):
    row_sum = history[-1]
    for u in range(start, start + size, chunk):
        part = pl.ds(u, chunk)
        gap = scores[part, :].reshape(-1, 8, peak.shape[1]) - paced(history, peak, pace)
        weight = jnp.exp2(gap * exp2_scale).reshape(chunk, peak.shape[1])
        if keep:
            scores[part, :] = weight
        weights[part, :] = weight.astype(jnp.bfloat16)
        row_sum = row_sum + fold_sum(weight)
        history.append(row_sum)


def spread_max(peak):
    return jnp.broadcast_to(jnp.max(peak, axis=0, keepdims=True), peak.shape)


def teacher_kernel(chips, rows, heads, info, q_ref, *refs):
    key_refs = refs[: 2 * chips]
    value_refs = refs[2 * chips : 4 * chips]
    proj_ref, out_ref, keys, values_t, query_t, *refs = refs[4 * chips :]
    scores, weights, (peaks, context) = refs[:2], refs[2:4], refs[4:]
    chip, core = info[0], info[1]
    wide = 2 * rows
    pairs = GROUP_T // 2
    for b in range(2 * chips):
        part = pl.ds(b * rows, rows)

        @pl.when(b < 2 * jnp.maximum(chip + 1, chips - 1))
        def _():
            for g in range(heads):
                columns = slice(g * HEAD, (g + 1) * HEAD)
                keys[g, part, :] = key_refs[b][:, columns]
                values_t[g, :, part] = value_refs[b][:, columns].T

    for h in range(heads * GROUP_T):
        half = pl.ds(h % 2 * rows, rows)
        query_t[h // 2, :, half] = q_ref[:, h * HEAD : (h + 1) * HEAD].T

    key_id = lax.broadcasted_iota(jnp.int32, (wide, wide), 0)
    row_id = lax.broadcasted_iota(jnp.int32, (wide, wide), 1)
    row_id = jnp.where(row_id < rows, row_id, row_id - rows)
    ahead = jnp.where(key_id < rows, key_id, key_id + (1 - 2 * core) * rows - rows)
    allowed = ahead <= row_id

    def score(b, pair, slot, peak):
        part = pl.ds(b * wide, wide)
        tile = dot(keys[pair // pairs, part, :], query_t[pair])
        if b == 0:
            tile = jnp.where(allowed, tile, floor_score)
        scores[slot][part, :] = tile
        return jnp.maximum(peak, held(b, fold_max(tile), floor_score))

    def held(b, value, otherwise):
        return value if b == 0 else jnp.where(b <= chip, value, otherwise)

    low = jnp.full((8, wide), floor_score, jnp.float32)

    for least, count in zip([0, *variants(chips)], variants(chips)):

        @pl.when(jnp.logical_and(chip >= least, chip < count))
        def _():
            peak = low
            for b in range(count):
                peak = score(b, 0, 0, peak)
            peaks[...] = peak

            def step(pair, slot):
                later = jnp.minimum(pair + 1, heads * pairs - 1)
                top = spread_max(peaks[...])
                history = [jnp.zeros((8, wide), jnp.float32)]
                peak = low
                for b in range(count):
                    bound = held(b, top, -floor_score)
                    weigh(scores[slot], weights[slot], b * wide, wide, bound, history, False, None)
                    peak = score(b, later, 1 - slot, peak)
                end = count * wide
                mixed = dot(values_t[pair // pairs, :, :end], weights[slot][:end, :])
                mixed = mixed / jnp.sum(history[-1], axis=0, keepdims=True)
                for half in range(2):
                    start = pl.multiple_of((2 * pair + half) * HEAD, HEAD)
                    made = mixed[:, half * rows : (half + 1) * rows]
                    context[pl.ds(start, HEAD), :] = made.astype(jnp.bfloat16)
                peaks[...] = peak

            def two(i, carried):
                step(2 * i, 0)
                step(2 * i + 1, 1)
                return carried

            lax.fori_loop(0, heads * pairs // 2, two, 0)

    deep = PER_TARGET * HEAD
    for t in range(heads * GROUP_T // PER_TARGET):
        made = dot(proj_ref[t].T, context[t * deep : (t + 1) * deep, :])
        out_ref[t * HEAD : (t + 1) * HEAD, :] = made.astype(jnp.bfloat16)


def teacher(info, queries, blocks, projection, first_head, heads):
    chips = len(blocks)
    rows = queries.shape[0]
    flat = [part for pair in blocks for part in pair]
    targets = heads * GROUP_T // PER_TARGET
    turn = first_head // heads
    in_specs = [pl.BlockSpec((rows, heads * GROUP_T * HEAD), lambda i, info: (0, turn))]
    in_specs += [pl.BlockSpec((rows, heads * HEAD), lambda i, info: (0, 0))] * len(flat)
    in_specs += [pl.BlockSpec((rows, heads * HEAD), lambda i, info: (0, 1))] * len(flat)
    in_specs += [
        pl.BlockSpec((targets, PER_TARGET * HEAD, HEAD), lambda i, info: (turn, 0, 0))
    ]
    wide = 2 * rows
    work = heads * GROUP_T * rows * chips * wide
    return pl.pallas_call(
        functools.partial(teacher_kernel, chips, rows, heads),
        out_shape=jax.ShapeDtypeStruct((targets * HEAD, rows), jnp.bfloat16),
        grid_spec=pltpu.PrefetchScalarGridSpec(
            num_scalar_prefetch=1,
            grid=(1,),
            in_specs=in_specs,
            out_specs=pl.BlockSpec((targets * HEAD, rows), lambda i, info: (0, 0)),
            scratch_shapes=[
                pltpu.VMEM((heads, chips * wide, HEAD), jnp.bfloat16),
                pltpu.VMEM((heads, HEAD, chips * wide), jnp.bfloat16),
                pltpu.VMEM((heads * GROUP_T // 2, HEAD, wide), jnp.bfloat16),
                *[pltpu.VMEM((chips * wide, wide), jnp.float32)] * 2,
                *[pltpu.VMEM((chips * wide, wide), jnp.bfloat16)] * 2,
                pltpu.VMEM((8, wide), jnp.float32),
                pltpu.VMEM((heads * GROUP_T * HEAD, rows), jnp.bfloat16),
            ],
        ),
        compiler_params=pltpu.CompilerParams(
            dimension_semantics=("arbitrary",), vmem_limit_bytes=vmem_limit
        ),
        cost_estimate=pl.CostEstimate(
            flops=4 * HEAD * work, bytes_accessed=4 * wide * HEAD * chips, transcendentals=work
        ),
        name="teacher",
    )(info, queries, *flat, *flat, projection)


def student_kernel(chips, rows, info, own_q_ref, far_q_ref, target_ref, *refs):
    key_refs = refs[: 2 * chips]
    value_refs = refs[2 * chips : 4 * chips]
    near_ref, away_ref, loss_ref, kept_ref, sent_ref = refs[4 * chips : 4 * chips + 5]
    keys, keys_t, values, values_t, query, query_t, scores, weights = refs[
        4 * chips + 5 : 4 * chips + 13
    ]
    grad_scores, key_sum, value_sum, query_sum, loss_sum = refs[4 * chips + 13 :]
    chip, core, bit = info[0], info[1], info[2]
    wide = 2 * rows
    half_rows = rows // 2
    for b in range(2 * chips):
        part = pl.ds(b * rows, rows)

        @pl.when(b < 2 * jnp.maximum(chip + 1, chips - 1))
        def _():
            key_block = key_refs[b][...]
            value_block = value_refs[b][...]
            keys[part, :] = key_block
            keys_t[:, part] = key_block.T
            values[part, :] = value_block
            values_t[:, part] = value_block.T
            key_sum[part, :] = jnp.zeros((rows, HEAD), jnp.float32)
            value_sum[part, :] = jnp.zeros((rows, HEAD), jnp.float32)

    mine = pl.multiple_of(bit * half_rows, half_rows)
    other = pl.multiple_of((1 - bit) * half_rows, half_rows)
    for h in range(GROUP_S):
        columns = slice(h * HEAD, (h + 1) * HEAD)
        base = h % 2 * rows
        query[h // 2, pl.ds(base + mine, half_rows), :] = own_q_ref[:, columns]
        query[h // 2, pl.ds(base + other, half_rows), :] = far_q_ref[:, columns]
    for p in range(GROUP_S // 2):
        query_t[p] = query[p].T

    key_id = lax.broadcasted_iota(jnp.int32, (wide, wide), 0)
    row_id = lax.broadcasted_iota(jnp.int32, (wide, wide), 1)
    row_id = jnp.where(row_id < rows, row_id, row_id - rows)
    within = jnp.where(key_id < rows, key_id, key_id - rows)
    place = jnp.where(within < half_rows, within + bit * half_rows, within - bit * half_rows)
    ahead = jnp.where(key_id < rows, place, place + (1 - 2 * core) * rows)
    allowed = ahead <= row_id
    loss_sum[...] = jnp.zeros_like(loss_sum)

    def held(b, value, otherwise):
        return value if b == 0 else jnp.where(b <= chip, value, otherwise)

    for least, count in zip([0, *variants(chips)], variants(chips)):

        @pl.when(jnp.logical_and(chip >= least, chip < count))
        def _():
            def step(pair, carried):
                end = count * wide
                peak = jnp.full((8, wide), floor_score, jnp.float32)
                for b in range(count):
                    part = pl.ds(b * wide, wide)
                    tile = dot(keys[part, :], query_t[pair])
                    if b == 0:
                        tile = jnp.where(allowed, tile, floor_score)
                    scores[part, :] = tile
                    peak = jnp.maximum(peak, held(b, fold_max(tile), floor_score))
                history = [jnp.zeros((8, wide), jnp.float32)]
                top = spread_max(peak)
                for b in range(count):
                    bound = held(b, top, -floor_score)
                    weigh(scores, weights, b * wide, wide, bound, history, True, 2)
                inverse = 1.0 / jnp.sum(history[-1], axis=0, keepdims=True)
                made = dot(values_t[:, :end], weights[:end, :]) * inverse
                start = pl.multiple_of(pair * 2 * HEAD, 2 * HEAD)
                target = target_ref[pl.ds(start, 2 * HEAD), :].astype(jnp.float32)
                mismatch = made - jnp.concatenate([target[:HEAD], target[HEAD:]], 1)
                squares = fold_sum(jnp.square(mismatch))
                loss_sum[...] += squares[:, :rows] + squares[:, rows:]
                delta = jnp.sum(mismatch * made, axis=0, keepdims=True)
                grad_t = mismatch.astype(jnp.bfloat16)
                grad = mismatch.T.astype(jnp.bfloat16)
                for u in range(0, end, piece):
                    part = pl.ds(u, piece)
                    prob = scores[part, :] * inverse
                    grad_prob = dot(values[part, :], grad_t)
                    grad_score = (prob * (grad_prob - delta)).astype(jnp.bfloat16)
                    grad_scores[part, :] = grad_score
                    key_sum[part, :] += dot(grad_score, query[pair])
                    value_sum[part, :] += dot(prob.astype(jnp.bfloat16), grad)
                summed = dot(keys_t[:, :end], grad_scores[:end, :]) * inverse_root
                query_sum[2 * pair] = summed[:, :rows].T
                query_sum[2 * pair + 1] = summed[:, rows:].T
                return carried

            lax.fori_loop(0, GROUP_S // 2, step, 0)

    for h in range(GROUP_S):
        near_ref[:, h * HEAD : (h + 1) * HEAD] = query_sum[h, pl.ds(mine, half_rows), :]
        away_ref[:, h * HEAD : (h + 1) * HEAD] = query_sum[h, pl.ds(other, half_rows), :].astype(
            jnp.bfloat16
        )
    loss_ref[...] = jnp.sum(loss_sum[...], axis=0, keepdims=True)
    for b in range(chips):

        @pl.when(b <= chip)
        def _():
            own = pl.ds(b * wide, rows)
            far = pl.ds(b * wide + rows, rows)
            kept_ref[b, :, :HEAD] = key_sum[own, :] * inverse_root
            kept_ref[b, :, HEAD:] = value_sum[own, :]
            sent_ref[b, :, :HEAD] = (key_sum[far, :] * inverse_root).astype(jnp.bfloat16)
            sent_ref[b, :, HEAD:] = value_sum[far, :].astype(jnp.bfloat16)


def student(info, own_queries, far_queries, target, blocks, pair, heads):
    chips = len(blocks)
    rows = blocks[0][0].shape[0]
    half_rows = rows // 2
    wide = 2 * rows
    flat = [part for both in blocks for part in both]
    width = GROUP_S * HEAD
    full = lambda i, info: (0, 0)
    in_specs = [
        pl.BlockSpec((half_rows, width), lambda i, info: (0, info[2] * heads + pair)),
        pl.BlockSpec((half_rows, width), lambda i, info: (0, pair)),
        pl.BlockSpec((width, rows), full),
    ]
    in_specs += [pl.BlockSpec((rows, HEAD), lambda i, info: (0, pair))] * len(flat)
    in_specs += [pl.BlockSpec((rows, HEAD), lambda i, info: (0, heads + pair))] * len(flat)
    work = GROUP_S * rows * chips * wide
    return pl.pallas_call(
        functools.partial(student_kernel, chips, rows),
        out_shape=(
            jax.ShapeDtypeStruct((half_rows, width), jnp.float32),
            jax.ShapeDtypeStruct((half_rows, width), jnp.bfloat16),
            jax.ShapeDtypeStruct((1, rows), jnp.float32),
            jax.ShapeDtypeStruct((chips, rows, 2 * HEAD), jnp.float32),
            jax.ShapeDtypeStruct((chips, rows, 2 * HEAD), jnp.bfloat16),
        ),
        grid_spec=pltpu.PrefetchScalarGridSpec(
            num_scalar_prefetch=1,
            grid=(1,),
            in_specs=in_specs,
            out_specs=(
                pl.BlockSpec((half_rows, width), full),
                pl.BlockSpec((half_rows, width), full),
                pl.BlockSpec((1, rows), full),
                pl.BlockSpec((chips, rows, 2 * HEAD), lambda i, info: (0, 0, 0)),
                pl.BlockSpec((chips, rows, 2 * HEAD), lambda i, info: (0, 0, 0)),
            ),
            scratch_shapes=[
                pltpu.VMEM((chips * wide, HEAD), jnp.bfloat16),
                pltpu.VMEM((HEAD, chips * wide), jnp.bfloat16),
                pltpu.VMEM((chips * wide, HEAD), jnp.bfloat16),
                pltpu.VMEM((HEAD, chips * wide), jnp.bfloat16),
                pltpu.VMEM((GROUP_S // 2, wide, HEAD), jnp.bfloat16),
                pltpu.VMEM((GROUP_S // 2, HEAD, wide), jnp.bfloat16),
                pltpu.VMEM((chips * wide, wide), jnp.float32),
                *[pltpu.VMEM((chips * wide, wide), jnp.bfloat16)] * 2,
                *[pltpu.VMEM((chips * wide, HEAD), jnp.float32)] * 2,
                pltpu.VMEM((GROUP_S, rows, HEAD), jnp.float32),
                pltpu.VMEM((8, rows), jnp.float32),
            ],
        ),
        compiler_params=pltpu.CompilerParams(
            dimension_semantics=("arbitrary",), vmem_limit_bytes=vmem_limit
        ),
        cost_estimate=pl.CostEstimate(
            flops=12 * HEAD * work, bytes_accessed=8 * wide * HEAD * chips, transcendentals=work
        ),
        name="student",
    )(info, own_queries, far_queries, target, *flat, *flat)


def program(
    teacher_query_array,
    teacher_keys,
    teacher_value_array,
    projection,
    student_query_array,
    student_keys,
    student_value_array,
):
    bit = lax.axis_index("section") % 2
    seq = lax.axis_index("seq")
    chips = lax.axis_size("seq") // 2
    info = jnp.stack([seq // 2, seq % 2, bit]).astype(jnp.int32)
    teacher_heads = TEACHER_KV_HEADS // 2
    student_heads = STUDENT_KV_HEADS // 2
    per_pair = teacher_heads // student_heads
    rows = teacher_keys.shape[1]
    half_rows = rows // 2

    def columns(array, which, width):
        return lax.dynamic_slice_in_dim(array, which * width, width, 1)

    kv_width = student_heads * HEAD
    q_width = STUDENT_Q_HEADS // 2 * HEAD
    own_q = student_query_array[0]

    def teacher_rows(pair):
        part = slice(pair * per_pair * HEAD, (pair + 1) * per_pair * HEAD)
        return jnp.concatenate([teacher_keys[0][:, part], teacher_value_array[0][:, part]], 1)

    def pair_rows(which):
        return jnp.concatenate(
            [
                columns(student_keys[0], which, kv_width),
                columns(student_value_array[0], which, kv_width),
            ],
            1,
        )

    far_rows = swap(pair_rows(1 - bit), "section")
    student_all = jnp.concatenate([pair_rows(bit), far_rows], 0)

    chunks = [spread(teacher_rows(pair), pair == 0) for pair in range(student_heads)]
    student_mine = spread(student_all)
    far_q = swap(columns(own_q, 1 - bit, q_width), "section")

    targets = []
    for pair in range(student_heads):
        blocks = both_cores(chunks[pair])
        made = teacher(
            info, teacher_query_array[0], blocks, projection[0], pair * per_pair, per_pair
        )
        targets.append(made)
    student_blocks = both_cores(student_mine)

    query_own, query_far, key_own, key_far, loss = [], [], [], [], 0.0
    for pair in range(student_heads):
        near, away, squares, kept, sent = student(
            info, own_q, far_q, targets[pair], student_blocks, pair, student_heads
        )
        query_own.append(near)
        query_far.append(swap(away, "section"))
        loss = loss + squares[0]
        terms = kept + swap(sent, "seq").astype(jnp.float32)
        summed = terms[0]
        for step in range(1, chips):
            got = back(terms[step].astype(jnp.bfloat16), step)
            summed = summed + got.astype(jnp.float32)
        far = swap(summed[half_rows:].astype(jnp.bfloat16), "section")
        key_own.append(summed[:half_rows])
        key_far.append(far.astype(jnp.float32))
    query_far = [part.astype(jnp.float32) for part in query_far]

    def arrange(own, far):
        return jnp.where(
            bit == 0,
            jnp.concatenate(own + far, 1),
            jnp.concatenate(far + own, 1),
        )

    grad_q = arrange(query_own, query_far)
    grad_k = arrange([x[:, :HEAD] for x in key_own], [x[:, :HEAD] for x in key_far])
    grad_v = arrange([x[:, HEAD:] for x in key_own], [x[:, HEAD:] for x in key_far])
    halves = loss.reshape(2, half_rows)
    mine = jnp.where(bit == 0, halves[0], halves[1])
    theirs = jnp.where(bit == 0, halves[1], halves[0])
    got = swap(theirs, "section")
    token_loss = (mine + got) / (STUDENT_Q_HEADS * HEAD)
    return grad_q[None], grad_k[None], grad_v[None], token_loss[None]


def solution(mesh):
    in_specs = (
        P("section", "seq", None),
        P("section", "seq", None),
        P("section", "seq", None),
        P("section", None, None, None),
        P("section", "seq", None),
        P("section", "seq", None),
        P("section", "seq", None),
    )
    out_specs = (
        P("section", "seq", None),
        P("section", "seq", None),
        P("section", "seq", None),
        P("section", "seq"),
    )
    return jax.shard_map(
        program, mesh=mesh, in_specs=in_specs, out_specs=out_specs, check_vma=False
    )
```
